32 devices in a mesh: groups: 2 (over x), seq: 16 (over z, y, core).
Axes of the slice: x: 2, y: 2, z: 4, core: 2. Of those that a mesh axis runs over, the one named last changes fastest.
Arguments:
- signal: bfloat16 [16384, 2048], P(('groups', 'seq')), parts along dimension 0, may hold values from -6 to 6
- gate_input: bfloat16 [16384, 2048], P(('groups', 'seq')), parts along dimension 0, may hold values from -6 to 6
- cotangent: bfloat16 [16384, 2048], P(('groups', 'seq')), parts along dimension 0, may hold values from -6 to 6
- block_factor: bfloat16 [512, 512], replicated, may hold values from -0.25 to 0.25
- cross_factor: bfloat16 [512, 16, 16], P('seq'), may hold values from -1.5 to 1.5
- order_table: int32 [512], replicated, may hold values from 0 to 511, each once
Outputs:
- grad_signal: bfloat16 [16384, 2048], P(('groups', 'seq')), parts along dimension 0
- grad_gate: bfloat16 [16384, 2048], P(('groups', 'seq')), parts along dimension 0
- grad_block: float32 [1024, 512], P('groups'), parts along dimension 0
- grad_cross: float32 [512, 32, 16], P('seq', 'groups'), parts along dimension 1
The draws below stay inside these ranges and needn't reach their ends.
There are 2 independent parts, one for each index of `groups`. The reference program is written for one: setup_inputs(seed, part) draws one part's arguments, and reference() takes and returns one part's arrays. A program takes and returns all parts, laid end to end along the dimension named above; an argument that names none is the same for every part. Nothing has to cross between parts.
Inputs may be any that keep to these rules, and one draw needn't show every extreme that they name: order_table holds every number of 0 to 511 exactly once.
All inputs are finite; a program needn't handle non-finite values.
Results may differ from the reference program's by a relative error of at most 0.0057.
Values may be sent and summed in bfloat16 or wider, within the bound.
A program may use at most 64 MiB of HBM per device.

```python
import math
import jax
import jax.numpy as jnp

BLOCK = 512
WIDTH = 2048
BLOCKS = 16
TOKENS = 8192


def shard_levels(key, extent, split, low, top_value):
    gain, own = 1.0, jax.random.fold_in(key, 6)
    for axis_at, parts in split:
        heights = jnp.exp(jax.random.uniform(jax.random.fold_in(own, axis_at), (parts,), jnp.float32, low / len(split), top_value / len(split)))
        gain = gain * jnp.repeat(heights, extent[axis_at] // parts).reshape([-1 if axis == axis_at else 1 for axis in range(len(extent))])
    return gain


def gaussian(key, shape, deviation, reach, pieces=(), dtype=jnp.bfloat16):
    gain = shard_levels(key, shape, pieces, -0.22, 0.18) if pieces else 1.0
    entries = jax.random.normal(key, shape, jnp.float32) * deviation * gain
    return jnp.minimum(jnp.maximum(entries, -reach), reach).astype(dtype)


def setup_inputs(seed: int = 0, part: int = 0) -> dict:
    key_list = jax.random.split(jax.random.key(seed), 7)
    own_keys = jax.random.split(jax.random.fold_in(key_list[6], part), 7)
    signal = gaussian(own_keys[0], (TOKENS, WIDTH), 1.0, 6.0, ((0, 16),))
    gate_input = gaussian(own_keys[1], (TOKENS, WIDTH), 1.0, 6.0, ((0, 16),))
    cotangent = gaussian(own_keys[2], (TOKENS, WIDTH), 1.0, 6.0, ((0, 16),))
    block_factor = gaussian(key_list[3], (BLOCK, BLOCK), BLOCK ** -0.5, 0.25)
    cross_factor = gaussian(key_list[4], (BLOCK, BLOCKS, BLOCKS), BLOCKS ** -0.5, 1.5, ((0, 16),))
    order_table = jax.random.permutation(key_list[5], BLOCK).astype(jnp.int32)
    return dict(signal=signal, gate_input=gate_input, cotangent=cotangent, block_factor=block_factor, cross_factor=cross_factor, order_table=order_table)


def reference(signal, gate_input, cotangent, block_factor, cross_factor, order_table):
    f32 = jnp.float32
    bf16 = jnp.bfloat16
    source = signal.reshape(BLOCKS, BLOCK, WIDTH)
    permuted = source[:, order_table, :]
    block_w = block_factor.astype(f32)
    cross_w = cross_factor.astype(f32)
    mixed = jnp.einsum('cb,abd->acd', block_w, permuted.astype(f32)).astype(bf16)
    gated = jnp.einsum('cij,jcd->icd', cross_w, mixed.astype(f32)).astype(bf16)
    cot = cotangent.astype(f32)
    gate_grad = (cot * gate_input.astype(f32)).astype(bf16).reshape(BLOCKS, BLOCK, WIDTH)
    grad_gate = (cot * gated.reshape(TOKENS, WIDTH).astype(f32)).astype(bf16)
    grad_cross = jnp.einsum('icd,jcd->cij', gate_grad.astype(f32), mixed.astype(f32)) / math.sqrt(WIDTH)
    back = jnp.einsum('cij,icd->jcd', cross_w, gate_grad.astype(f32)).astype(bf16)
    grad_block = jnp.einsum('acd,abd->cb', back.astype(f32), permuted.astype(f32)) / math.sqrt(BLOCKS * WIDTH)
    spread = jnp.einsum('cb,acd->abd', block_w, back.astype(f32)).astype(bf16)
    grad_signal = jnp.zeros_like(spread).at[:, order_table, :].set(spread).reshape(TOKENS, WIDTH)
    return (grad_signal, grad_gate, grad_block, grad_cross)
```

```python
import functools
import math

import jax
import jax.numpy as jnp
from jax import lax
from jax.experimental import pallas as pl
from jax.experimental.pallas import tpu as pltpu
from jax.sharding import PartitionSpec as P

LAYER = 4


def log2(value):
    return value.bit_length() - 1


def dot(a, b, ca, cb):
    return lax.dot_general(a, b, (((ca,), (cb,)), ((), ())), preferred_element_type=jnp.float32)


def iota(shape, dim):
    return lax.broadcasted_iota(jnp.int32, shape, dim)


def exchange_kernel(
    n, sig, gate, cot, bf, crs, order,
    out_sig, out_gate, out_block, out_cross,
    gg, mx, pm, bk, gt, rg, rm, rb, rt, pt, bp, wf, pb, s1, ls, s2, gb,
    send, recv, ar_send, ar_recv,
):
    f32, bf16 = jnp.float32, jnp.bfloat16
    me = lax.axis_index("seq")
    block, width = sig.shape
    rows = block // n
    tile = min(512, width)
    tiles = width // tile
    nz = n // LAYER
    lrows, zrows = block // LAYER, block // n
    zz, qq = lax.div(me, LAYER), lax.rem(me, LAYER)

    def at(index, size=rows):
        return pl.ds(pl.multiple_of(index * size, size), size)

    def peer(k):
        return lax.rem(me + k, n)

    def copy(phase, k, src, dst):
        return pltpu.make_async_remote_copy(
            src_ref=src.at[at(peer(k))],
            dst_ref=dst.at[at(me)],
            send_sem=send.at[phase, k - 1],
            recv_sem=recv.at[phase, k - 1],
            device_id={"seq": peer(k)},
            device_id_type=pl.DeviceIdType.MESH,
        )

    def each(body):
        def step(k, carry):
            body(k)
            return carry
        lax.fori_loop(1, n, step, 0)

    def columns(body):
        def step(t, carry):
            body(pl.ds(pl.multiple_of(t * tile, tile), tile))
            return carry
        lax.fori_loop(0, tiles, step, 0)

    def own(src, dst):
        dst[at(me), :] = src[at(me), :]

    barrier = pltpu.get_barrier_semaphore()
    each(lambda k: pl.semaphore_signal(
        barrier, inc=1, device_id={"seq": peer(k)}, device_id_type=pl.DeviceIdType.MESH))
    pl.semaphore_wait(barrier, n - 1)

    def multiply(r):
        gg[r, :] = (cot[r, :].astype(f32) * gate[r, :].astype(f32)).astype(bf16)

    def first(k):
        multiply(at(peer(k)))
        copy(0, k, gg, rg).start()

    each(first)
    multiply(at(me))
    own(gg, rg)

    pt[...] = jnp.where(iota((block, block), 0) == order[...], 1.0, 0.0).astype(bf16)
    bp[...] = dot(bf[...], pt[...], 1, 1).astype(bf16)

    def mix(c):
        mx[:, c] = dot(bp[...], sig[:, c], 1, 0).astype(bf16)

    columns(mix)
    each(lambda k: copy(1, k, mx, rm).start())
    own(mx, rm)

    def permute(c):
        pm[:, c] = dot(pt[...], sig[:, c], 0, 0).astype(bf16)

    columns(permute)

    sr, sn = log2(rows), log2(n)
    spread = jnp.where(
        iota((rows, block), 0) == (iota((rows, block), 1) & (rows - 1)), 1.0, 0.0).astype(bf16)
    wide = dot(crs[...], spread, 1, 0)
    keep = (iota((n * n, block), 0) & (n - 1)) == (iota((n * n, block), 1) >> sr)
    picked = jnp.where(keep, wide, 0.0).astype(bf16)
    rise = jnp.where(
        (iota((block, n * n), 0) >> sr) == (iota((block, n * n), 1) >> sn), 1.0, 0.0).astype(bf16)
    tall = dot(rise, picked, 1, 0)
    same = (iota((block, block), 0) & (rows - 1)) == (iota((block, block), 1) & (rows - 1))
    wf[...] = jnp.where(same, tall, 0.0).astype(bf16)

    each(lambda k: copy(0, k, gg, rg).wait_recv())

    def backward(c):
        bk[:, c] = dot(wf[...], rg[:, c], 0, 0).astype(bf16)

    columns(backward)
    each(lambda k: copy(2, k, bk, rb).start())
    own(bk, rb)

    each(lambda k: copy(1, k, mx, rm).wait_recv())

    def forward(c):
        gt[:, c] = dot(wf[...], rm[:, c], 1, 0).astype(bf16)

    columns(forward)
    each(lambda k: copy(3, k, gt, rt).start())
    own(gt, rt)

    half = block // 2
    for h in range(2):
        pairs = dot(rg[pl.ds(h * half, half), :], rm[...], 1, 1)
        match = (iota((half, block), 0) & (rows - 1)) == (iota((half, block), 1) & (rows - 1))
        pairs = jnp.where(match, pairs, 0.0).reshape(half // rows, rows, block)
        out_cross[pl.ds(h * (n // 2), n // 2), :] = pairs.sum(axis=1) * (1.0 / math.sqrt(width))

    def layer_peer(d):
        return lax.rem(qq + d, LAYER)

    def z_peer(d):
        return lax.rem(zz + d, nz)

    def ar_copy(stage, d, src, dst, device):
        return pltpu.make_async_remote_copy(
            src_ref=src, dst_ref=dst,
            send_sem=ar_send.at[stage, d - 1], recv_sem=ar_recv.at[stage, d - 1],
            device_id={"seq": device}, device_id_type=pl.DeviceIdType.MESH,
        )

    each(lambda k: copy(2, k, bk, rb).wait_recv())
    pb[...] = dot(rb[...], pm[...], 1, 1)
    one = [ar_copy(0, d, pb.at[at(layer_peer(d), lrows)], s1.at[d - 1], zz * LAYER + layer_peer(d))
           for d in range(1, LAYER)]
    for c in one:
        c.start()

    def back_signal(c):
        out_sig[:, c] = dot(bp[...], rb[:, c], 0, 0).astype(bf16)

    columns(back_signal)
    for c in one:
        c.wait_recv()
    ls[...] = pb[at(qq, lrows), :] + s1[0] + s1[1] + s1[2]
    two = [ar_copy(1, d, ls.at[at(z_peer(d), zrows)], s2.at[d - 1], z_peer(d) * LAYER + qq)
           for d in range(1, nz)]
    for c in two:
        c.start()
    for c in two:
        c.wait_recv()
    total = ls[at(zz, zrows), :]
    for d in range(nz - 1):
        total = total + s2[d]
    mine = at(qq * nz + zz, zrows)
    gb[mine, :] = total * (1.0 / math.sqrt(n * width))
    three = [ar_copy(2, d, gb.at[mine], gb.at[mine], z_peer(d) * LAYER + qq) for d in range(1, nz)]
    for c in three:
        c.start()
    for c in three:
        c.wait_recv()
    layer = at(qq, lrows)
    four = [ar_copy(3, d, gb.at[layer], gb.at[layer], zz * LAYER + layer_peer(d))
            for d in range(1, LAYER)]
    for c in four:
        c.start()

    def finish(r):
        out_gate[r, :] = (cot[r, :].astype(f32) * rt[r, :].astype(f32)).astype(bf16)

    finish(at(me))

    def last(k):
        copy(3, k, gt, rt).wait_recv()
        finish(at(lax.rem(me + n - k, n)))

    each(last)
    for c in four:
        c.wait_recv()
    out_block[...] = gb[...]

    def drain(k):
        copy(0, k, gg, rg).wait_send()
        copy(1, k, mx, rm).wait_send()
        copy(2, k, bk, rb).wait_send()
        copy(3, k, gt, rt).wait_send()

    each(drain)
    for c in one + two + three + four:
        c.wait_send()


def fused(signal, gate_input, cotangent, block_factor, cross_factor, order_table):
    f32, bf16 = jnp.float32, jnp.bfloat16
    n = lax.axis_size("seq")
    block, width = signal.shape
    rows = block // n
    nz = n // LAYER
    crs = cross_factor.transpose(1, 2, 0).reshape(n * n, rows)
    full = pltpu.VMEM((block, width), bf16)
    square = pltpu.VMEM((block, block), bf16)
    vmem = pl.BlockSpec(memory_space=pltpu.VMEM)
    grad_signal, grad_gate, grad_block, pairs = pl.pallas_call(
        functools.partial(exchange_kernel, n),
        out_shape=(
            jax.ShapeDtypeStruct((block, width), bf16),
            jax.ShapeDtypeStruct((block, width), bf16),
            jax.ShapeDtypeStruct((block, block), f32),
            jax.ShapeDtypeStruct((n, block), f32),
        ),
        in_specs=[vmem] * 6,
        out_specs=(vmem,) * 4,
        scratch_shapes=[full] * 9 + [square] * 3 + [
            pltpu.VMEM((block, block), f32),
            pltpu.VMEM((LAYER - 1, block // LAYER, block), f32),
            pltpu.VMEM((block // LAYER, block), f32),
            pltpu.VMEM((nz - 1, block // n, block), f32),
            pltpu.VMEM((block, block), f32),
            pltpu.SemaphoreType.DMA((4, n - 1)),
            pltpu.SemaphoreType.DMA((4, n - 1)),
            pltpu.SemaphoreType.DMA((4, max(LAYER, nz) - 1)),
            pltpu.SemaphoreType.DMA((4, max(LAYER, nz) - 1)),
        ],
        compiler_params=pltpu.CompilerParams(
            collective_id=0, has_side_effects=True, vmem_limit_bytes=56 << 20),
    )(signal, gate_input, cotangent, block_factor, crs, order_table.reshape(1, block))
    grad_cross = pairs.reshape(n, n, rows).transpose(2, 0, 1)
    return (grad_signal, grad_gate, grad_block, grad_cross)


def per_device(signal, gate_input, cotangent, block_factor, cross_factor, order_table):
    f32 = jnp.float32
    bf16 = jnp.bfloat16
    count = lax.axis_size("seq")
    width = signal.shape[1]
    permuted = jnp.take(signal, order_table, axis=0)
    mixed = jnp.dot(block_factor, permuted, preferred_element_type=f32).astype(bf16)
    gate_grad = (cotangent.astype(f32) * gate_input.astype(f32)).astype(bf16)
    spread_mixed = lax.all_to_all(mixed[None], "seq", split_axis=1, concat_axis=0, tiled=True)
    spread_grad = lax.all_to_all(gate_grad[None], "seq", split_axis=1, concat_axis=0, tiled=True)
    gated = jnp.einsum(
        "cij,jcd->icd", cross_factor, spread_mixed, preferred_element_type=f32
    ).astype(bf16)
    gated_home = lax.all_to_all(gated, "seq", split_axis=0, concat_axis=1, tiled=True)
    grad_cross = jnp.einsum(
        "icd,jcd->cij", spread_grad, spread_mixed, preferred_element_type=f32
    ) / math.sqrt(width)
    back = jnp.einsum("cij,icd->jcd", cross_factor, spread_grad, preferred_element_type=f32).astype(
        bf16
    )
    back_home = lax.all_to_all(back, "seq", split_axis=0, concat_axis=1, tiled=True)
    grad_gate = (cotangent.astype(f32) * gated_home[0].astype(f32)).astype(bf16)
    back_rows = back_home[0]
    partial_block = lax.dot_general(
        back_rows, permuted, (((1,), (1,)), ((), ())), preferred_element_type=f32
    )
    grad_block = lax.psum(partial_block, "seq") / math.sqrt(count * width)
    spread = lax.dot_general(
        block_factor, back_rows, (((0,), (0,)), ((), ())), preferred_element_type=f32
    ).astype(bf16)
    grad_signal = jnp.zeros_like(spread).at[order_table].set(spread)
    return (grad_signal, grad_gate, grad_block, grad_cross)


def solution(mesh):
    in_specs = (
        P(("groups", "seq"), None),
        P(("groups", "seq"), None),
        P(("groups", "seq"), None),
        P(),
        P("seq", None, None),
        P(),
    )
    out_specs = (
        P(("groups", "seq"), None),
        P(("groups", "seq"), None),
        P("groups", None),
        P("seq", "groups", None),
    )

    def body(signal, *rest):
        n = mesh.shape["seq"]
        block = signal.shape[0]
        whole = block % n == 0 and (block // n) % 16 == 0 and n % (2 * LAYER) == 0
        whole = whole and n & (n - 1) == 0 and block & (block - 1) == 0
        return (fused if whole else per_device)(signal, *rest)

    return jax.shard_map(body, mesh=mesh, in_specs=in_specs, out_specs=out_specs, check_vma=False)
```

```python
import functools
import math

import jax
import jax.numpy as jnp
from jax import lax
from jax.experimental import pallas as pl
from jax.experimental.pallas import tpu as pltpu
from jax.sharding import PartitionSpec as P

LAYER = 4


def log2(value):
    return value.bit_length() - 1


def dot(a, b, ca, cb):
    return lax.dot_general(a, b, (((ca,), (cb,)), ((), ())), preferred_element_type=jnp.float32)


def iota(shape, dim):
    return lax.broadcasted_iota(jnp.int32, shape, dim)


def exchange_kernel(
    n, gate_in, cot_in, sig_in, order_in, bf_in, crs_in,
    out_sig, out_gate, out_block, out_cross,
    gate, cot, sig, order, bf, crs,
    gg, mx, pm, bk, gt, rg, rm, rb, rt, os, pt, bp, wf,
    pb, s1, ls, s2, ms, s3, gb, gc, send, recv, ar_send, ar_recv, local, closing,
):
    f32, bf16 = jnp.float32, jnp.bfloat16
    me = lax.axis_index("seq")
    block, width = sig.shape
    rows = block // n
    half = width // 2
    tile = min(512, half)
    nz = n // LAYER
    lrows, zrows = block // LAYER, block // LAYER // 2
    zz, qq = lax.div(me, LAYER), lax.rem(me, LAYER)
    left, right, whole = (0, half), (half, half), (0, width)

    def at(index, size=rows):
        return pl.ds(pl.multiple_of(index * size, size), size)

    def peer(k):
        return lax.rem(me + k, n)

    def remote(phase, k):
        src, dst, (start, size) = phases[phase]
        return pltpu.make_async_remote_copy(
            src_ref=src.at[at(peer(k)), pl.ds(start, size)],
            dst_ref=dst.at[at(me), pl.ds(start, size)],
            send_sem=send.at[phase, k - 1],
            recv_sem=recv.at[phase, k - 1],
            device_id={"seq": peer(k)},
            device_id_type=pl.DeviceIdType.MESH,
        )

    phases = [(gg, rg, whole), (mx, rm, left), (bk, rb, whole), (mx, rm, right),
              (gt, rt, left), (gt, rt, right)]

    def each(body):
        def step(k, carry):
            body(k)
            return carry
        lax.fori_loop(1, n, step, 0)

    def columns(part, body):
        def step(t, carry):
            body(pl.ds(pl.multiple_of(part[0] + t * tile, tile), tile))
            return carry
        lax.fori_loop(0, part[1] // tile, step, 0)

    def own(src, dst):
        dst[at(me), :] = src[at(me), :]

    def follow(phase):
        def step(k):
            if phase > 1:
                remote(phase - 2, k).wait_send()
            remote(phase, k).start()
        each(step)

    def arrive(phase):
        each(lambda k: remote(phase, k).wait_recv())

    loads = [pltpu.make_async_copy(src, dst, local.at[i])
             for i, (src, dst) in enumerate([(gate_in, gate), (cot_in, cot), (sig_in, sig),
                                             (order_in, order), (bf_in, bf), (crs_in, crs)])]
    for c in loads:
        c.start()
    barrier = pltpu.get_barrier_semaphore()
    each(lambda k: pl.semaphore_signal(
        barrier, inc=1, device_id={"seq": peer(k)}, device_id_type=pl.DeviceIdType.MESH))
    loads[0].wait()
    loads[1].wait()
    pl.semaphore_wait(barrier, n - 1)

    def multiply(r):
        gg[r, :] = (cot[r, :].astype(f32) * gate[r, :].astype(f32)).astype(bf16)

    def first(k):
        multiply(at(peer(k)))
        remote(0, k).start()

    each(first)
    multiply(at(me))
    own(gg, rg)

    for c in loads[2:]:
        c.wait()
    pt[...] = jnp.where(iota((block, block), 0) == order[...], 1.0, 0.0).astype(bf16)
    bp[...] = dot(bf[...], pt[...], 1, 1).astype(bf16)

    def mix(c):
        mx[:, c] = dot(bp[...], sig[:, c], 1, 0).astype(bf16)
        pm[:, c] = dot(pt[...], sig[:, c], 0, 0).astype(bf16)

    columns(whole, mix)
    own(mx, rm)

    sr, sn = log2(rows), log2(n)
    spread = jnp.where(
        iota((rows, block), 0) == (iota((rows, block), 1) & (rows - 1)), 1.0, 0.0)
    keep = (iota((n * n, block), 0) & (n - 1)) == (iota((n * n, block), 1) >> sr)
    picked = jnp.where(keep, dot(crs[...], spread.astype(bf16), 1, 0), 0.0).astype(bf16)
    rise = jnp.where(
        (iota((block, n * n), 0) >> sr) == (iota((block, n * n), 1) >> sn), 1.0, 0.0).astype(bf16)
    same = (iota((block, block), 0) & (rows - 1)) == (iota((block, block), 1) & (rows - 1))
    wf[...] = jnp.where(same, dot(rise, picked, 1, 0), 0.0).astype(bf16)

    follow(1)

    arrive(0)

    def backward(c):
        bk[:, c] = dot(wf[...], rg[:, c], 0, 0).astype(bf16)

    columns(whole, backward)
    own(bk, rb)
    follow(2)

    def forward(c):
        gt[:, c] = dot(wf[...], rm[:, c], 1, 0).astype(bf16)

    arrive(1)
    columns(left, forward)
    follow(3)

    def layer_peer(d):
        return lax.rem(qq + d, LAYER)

    def z_peer(bit):
        size = 1 << bit
        other = zz + size - 2 * size * lax.rem(lax.div(zz, size), 2)
        return other * LAYER + qq

    def ar_copy(stage, d, src, dst, device):
        return pltpu.make_async_remote_copy(
            src_ref=src, dst_ref=dst,
            send_sem=ar_send.at[stage, d - 1], recv_sem=ar_recv.at[stage, d - 1],
            device_id={"seq": device}, device_id_type=pl.DeviceIdType.MESH,
        )

    arrive(2)
    pb[...] = dot(rb[...], pm[...], 1, 1)
    one = [ar_copy(0, d, pb.at[at(layer_peer(d), lrows)], s1.at[d - 1], zz * LAYER + layer_peer(d))
           for d in range(1, LAYER)]
    for c in one:
        c.start()

    def back_signal(c):
        os[:, c] = dot(bp[...], rb[:, c], 0, 0).astype(bf16)

    columns(whole, back_signal)
    store_sig = pltpu.make_async_copy(os, out_sig, local.at[0])
    store_sig.start()
    for c in one:
        c.wait_recv()
    ls[...] = pb[at(qq, lrows), :] + s1[0] + s1[1] + s1[2]
    even = lax.rem(zz, 2)
    two = [ar_copy(1, 1, ls.at[at(1 - even, zrows)], s2, z_peer(0))]
    two[0].start()

    follow(4)

    two[0].wait_recv()
    ms[0] = ls[at(even, zrows), :] + s2[...]

    def swap(bit):
        return ar_copy(1 + bit, 1, ms.at[bit - 1], s3.at[bit - 1], z_peer(bit))

    swaps = [swap(bit) for bit in range(1, log2(nz))]
    swaps[0].start()

    arrive(3)
    columns(right, forward)
    own(gt, rt)
    follow(5)

    for i, c in enumerate(swaps):
        c.wait_recv()
        ms[i + 1] = ms[i] + s3[i]
        if i + 1 < len(swaps):
            swaps[i + 1].start()
    mine = at(qq * 2 + even, zrows)
    gb[mine, :] = ms[len(swaps)] * (1.0 / math.sqrt(n * width))
    after = 1 + log2(nz)
    three = [ar_copy(after, 1, gb.at[mine], gb.at[mine], z_peer(0))]
    three[0].start()

    hb = block // 2
    for h in range(2):
        pairs = dot(rg[pl.ds(h * hb, hb), :], rm[...], 1, 1)
        match = (iota((hb, block), 0) & (rows - 1)) == (iota((hb, block), 1) & (rows - 1))
        pairs = jnp.where(match, pairs, 0.0).reshape(hb // rows, rows, block).sum(axis=1)
        pairs = jnp.broadcast_to(pairs[:, None, :], (n // 2, n, block)).reshape(n * n // 2, block)
        pairs = jnp.where(keep[: n * n // 2], pairs, 0.0)
        narrow = lax.dot_general(
            pairs, spread, (((1,), (1,)), ((), ())),
            precision=lax.Precision.HIGHEST, preferred_element_type=f32)
        gc[pl.ds(h * (n * n // 2), n * n // 2), :] = narrow * (1.0 / math.sqrt(width))
    store_cross = pltpu.make_async_copy(gc, out_cross, local.at[1])
    store_cross.start()
    three[0].wait_recv()
    layer = at(qq, lrows)
    four = [ar_copy(after + 1, d, gb.at[layer], gb.at[layer], zz * LAYER + layer_peer(d))
            for d in range(1, LAYER)]
    for c in four:
        c.start()

    def finish(r, part):
        c = pl.ds(*part)
        rt[r, c] = (cot[r, c].astype(f32) * rt[r, c].astype(f32)).astype(bf16)

    def close(phase):
        part = phases[phase][2]
        finish(at(me), part)
        stored(phase, 0).start()

        def last(k):
            remote(phase, k).wait_recv()
            finish(at(lax.rem(me + n - k, n)), part)
            stored(phase, k).start()

        each(last)

    def stored(phase, k):
        r, c = at(lax.rem(me + n - k, n)), pl.ds(*phases[phase][2])
        return pltpu.make_async_copy(rt.at[r, c], out_gate.at[r, c], closing.at[phase - 4, k])

    close(4)
    for c in four:
        c.wait_recv()
    store_block = pltpu.make_async_copy(gb, out_block, local.at[2])
    store_block.start()
    close(5)

    def drain(k):
        for phase in (4, 5):
            remote(phase, k).wait_send()
            stored(phase, k).wait()

    for phase in (4, 5):
        stored(phase, 0).wait()
    each(drain)
    for c in one + two + swaps + three + four:
        c.wait_send()
    for c in (store_sig, store_cross, store_block):
        c.wait()


def write_kernel(count, *refs):
    copies = [pltpu.make_async_copy(src, dst, refs[-1].at[i])
              for i, (src, dst) in enumerate(zip(refs[:count], refs[count:]))]
    for c in copies:
        c.start()
    for c in copies:
        c.wait()


def write(*arrays):
    free = pl.BlockSpec(memory_space=pl.ANY)
    return pl.pallas_call(
        functools.partial(write_kernel, len(arrays)),
        out_shape=tuple(jax.ShapeDtypeStruct(x.shape, x.dtype) for x in arrays),
        in_specs=[free] * len(arrays),
        out_specs=(free,) * len(arrays),
        scratch_shapes=[pltpu.SemaphoreType.DMA((len(arrays),))],
        compiler_params=pltpu.CompilerParams(vmem_limit_bytes=1 << 20),
    )(*arrays)


def fused(signal, gate_input, cotangent, block_factor, cross_factor, order_table):
    f32, bf16 = jnp.float32, jnp.bfloat16
    n = lax.axis_size("seq")
    block, width = signal.shape
    rows = block // n
    nz = n // LAYER
    crs = cross_factor.transpose(1, 2, 0).reshape(n * n, rows)
    full = pltpu.VMEM((block, width), bf16)
    square = pltpu.VMEM((block, block), bf16)
    free = pl.BlockSpec(memory_space=pl.ANY)
    inputs = (gate_input, cotangent, signal, order_table.reshape(1, block), block_factor, crs)
    steps = 3 + log2(nz)
    results = pl.pallas_call(
        functools.partial(exchange_kernel, n),
        out_shape=(
            jax.ShapeDtypeStruct((block, width), bf16),
            jax.ShapeDtypeStruct((block, width), bf16),
            jax.ShapeDtypeStruct((block, block), f32),
            jax.ShapeDtypeStruct((n * n, rows), f32),
        ),
        in_specs=[pl.BlockSpec(memory_space=pltpu.HBM)] * 6,
        out_specs=(free,) * 4,
        scratch_shapes=[pltpu.VMEM(x.shape, x.dtype) for x in inputs]
        + [full] * 10 + [square] * 3 + [
            pltpu.VMEM((block, block), f32),
            pltpu.VMEM((LAYER - 1, block // LAYER, block), f32),
            pltpu.VMEM((block // LAYER, block), f32),
            pltpu.VMEM((block // LAYER // 2, block), f32),
            pltpu.VMEM((log2(nz), block // LAYER // 2, block), f32),
            pltpu.VMEM((log2(nz) - 1, block // LAYER // 2, block), f32),
            pltpu.VMEM((block, block), f32),
            pltpu.VMEM((n * n, rows), f32),
            pltpu.SemaphoreType.DMA((6, n - 1)),
            pltpu.SemaphoreType.DMA((6, n - 1)),
            pltpu.SemaphoreType.DMA((steps, LAYER - 1)),
            pltpu.SemaphoreType.DMA((steps, LAYER - 1)),
            pltpu.SemaphoreType.DMA((6,)),
            pltpu.SemaphoreType.DMA((2, n)),
        ],
        compiler_params=pltpu.CompilerParams(
            collective_id=0, has_side_effects=True, vmem_limit_bytes=40 << 20),
    )(*(pltpu.with_memory_space_constraint(x, pltpu.HBM) for x in inputs))
    grad_signal, grad_gate, grad_block, pairs = write(*results)
    grad_cross = pairs.reshape(n, n, rows).transpose(2, 0, 1)
    return (grad_signal, grad_gate, grad_block, grad_cross)


def per_device(signal, gate_input, cotangent, block_factor, cross_factor, order_table):
    f32 = jnp.float32
    bf16 = jnp.bfloat16
    count = lax.axis_size("seq")
    width = signal.shape[1]
    permuted = jnp.take(signal, order_table, axis=0)
    mixed = jnp.dot(block_factor, permuted, preferred_element_type=f32).astype(bf16)
    gate_grad = (cotangent.astype(f32) * gate_input.astype(f32)).astype(bf16)
    spread_mixed = lax.all_to_all(mixed[None], "seq", split_axis=1, concat_axis=0, tiled=True)
    spread_grad = lax.all_to_all(gate_grad[None], "seq", split_axis=1, concat_axis=0, tiled=True)
    gated = jnp.einsum(
        "cij,jcd->icd", cross_factor, spread_mixed, preferred_element_type=f32
    ).astype(bf16)
    gated_home = lax.all_to_all(gated, "seq", split_axis=0, concat_axis=1, tiled=True)
    grad_cross = jnp.einsum(
        "icd,jcd->cij", spread_grad, spread_mixed, preferred_element_type=f32
    ) / math.sqrt(width)
    back = jnp.einsum("cij,icd->jcd", cross_factor, spread_grad, preferred_element_type=f32).astype(
        bf16
    )
    back_home = lax.all_to_all(back, "seq", split_axis=0, concat_axis=1, tiled=True)
    grad_gate = (cotangent.astype(f32) * gated_home[0].astype(f32)).astype(bf16)
    back_rows = back_home[0]
    partial_block = lax.dot_general(
        back_rows, permuted, (((1,), (1,)), ((), ())), preferred_element_type=f32
    )
    grad_block = lax.psum(partial_block, "seq") / math.sqrt(count * width)
    spread = lax.dot_general(
        block_factor, back_rows, (((0,), (0,)), ((), ())), preferred_element_type=f32
    ).astype(bf16)
    grad_signal = jnp.zeros_like(spread).at[order_table].set(spread)
    return (grad_signal, grad_gate, grad_block, grad_cross)


def solution(mesh):
    in_specs = (
        P(("groups", "seq"), None),
        P(("groups", "seq"), None),
        P(("groups", "seq"), None),
        P(),
        P("seq", None, None),
        P(),
    )
    out_specs = (
        P(("groups", "seq"), None),
        P(("groups", "seq"), None),
        P("groups", None),
        P("seq", "groups", None),
    )

    def body(signal, *rest):
        n = mesh.shape["seq"]
        block = signal.shape[0]
        whole = block % n == 0 and (block // n) % 16 == 0 and n % (4 * LAYER) == 0
        whole = whole and n & (n - 1) == 0 and block & (block - 1) == 0
        return (fused if whole else per_device)(signal, *rest)

    return jax.shard_map(body, mesh=mesh, in_specs=in_specs, out_specs=out_specs, check_vma=False)
```

```python
import functools
import math

import jax
import jax.numpy as jnp
from jax import lax
from jax.experimental import pallas as pl
from jax.experimental.pallas import tpu as pltpu
from jax.sharding import PartitionSpec as P

LAYER = 4


def log2(value):
    return value.bit_length() - 1


def dot(a, b, ca, cb):
    return lax.dot_general(a, b, (((ca,), (cb,)), ((), ())), preferred_element_type=jnp.float32)


def iota(shape, dim):
    return lax.broadcasted_iota(jnp.int32, shape, dim)


def exchange_kernel(
    n, gate_in, cot_in, sig_in, order_in, bf_in, crs_in,
    out_sig, out_gate, out_block, out_cross,
    gate, cot, sig, order, bf, crs,
    gg, mx, pm, bk, gt, rg, rm, rb, rt, os, pt, bp, wf,
    pb, s1, ls, s2, ms, s3, gb, gc, send, recv, ar_send, ar_recv, local, closing,
):
    f32, bf16 = jnp.float32, jnp.bfloat16
    me = lax.axis_index("seq")
    block, width = sig.shape
    rows = block // n
    half = width // 2
    tile = min(512, half)
    nz = n // LAYER
    lrows, zrows = block // LAYER, block // LAYER // 2
    zz, qq = lax.div(me, LAYER), lax.rem(me, LAYER)
    left, right, whole = (0, half), (half, half), (0, width)

    def at(index, size=rows):
        return pl.ds(pl.multiple_of(index * size, size), size)

    def peer(k):
        return lax.rem(me + k, n)

    def remote(phase, k):
        src, dst, (start, size) = phases[phase]
        return pltpu.make_async_remote_copy(
            src_ref=src.at[at(peer(k)), pl.ds(start, size)],
            dst_ref=dst.at[at(me), pl.ds(start, size)],
            send_sem=send.at[phase, k - 1],
            recv_sem=recv.at[phase, k - 1],
            device_id={"seq": peer(k)},
            device_id_type=pl.DeviceIdType.MESH,
        )

    phases = [(gg, rg, whole), (mx, rm, left), (bk, rb, whole), (mx, rm, right),
              (gt, rt, left), (gt, rt, right)]

    def each(body):
        def step(k, carry):
            body(k)
            return carry
        lax.fori_loop(1, n, step, 0)

    def columns(part, body):
        def step(t, carry):
            body(pl.ds(pl.multiple_of(part[0] + t * tile, tile), tile))
            return carry
        lax.fori_loop(0, part[1] // tile, step, 0)

    def own(src, dst):
        dst[at(me), :] = src[at(me), :]

    def follow(phase):
        def step(k):
            if phase > 1:
                remote(phase - 2, k).wait_send()
            remote(phase, k).start()
        each(step)

    def arrive(phase):
        each(lambda k: remote(phase, k).wait_recv())

    loads = [pltpu.make_async_copy(src, dst, local.at[i])
             for i, (src, dst) in enumerate([(gate_in, gate), (cot_in, cot), (sig_in, sig),
                                             (order_in, order), (bf_in, bf), (crs_in, crs)])]
    for c in loads:
        c.start()
    barrier = pltpu.get_barrier_semaphore()
    each(lambda k: pl.semaphore_signal(
        barrier, inc=1, device_id={"seq": peer(k)}, device_id_type=pl.DeviceIdType.MESH))
    loads[0].wait()
    loads[1].wait()
    pl.semaphore_wait(barrier, n - 1)

    def multiply(r):
        gg[r, :] = (cot[r, :].astype(f32) * gate[r, :].astype(f32)).astype(bf16)

    def first(k):
        multiply(at(peer(k)))
        remote(0, k).start()

    each(first)
    multiply(at(me))
    own(gg, rg)

    for c in loads[2:]:
        c.wait()
    pt[...] = jnp.where(iota((block, block), 0) == order[...], 1.0, 0.0).astype(bf16)
    bp[...] = dot(bf[...], pt[...], 1, 1).astype(bf16)

    def mix(c):
        mx[:, c] = dot(bp[...], sig[:, c], 1, 0).astype(bf16)
        pm[:, c] = dot(pt[...], sig[:, c], 0, 0).astype(bf16)

    columns(whole, mix)
    own(mx, rm)

    sr, sn = log2(rows), log2(n)
    spread = jnp.where(
        iota((rows, block), 0) == (iota((rows, block), 1) & (rows - 1)), 1.0, 0.0)
    keep = (iota((n * n, block), 0) & (n - 1)) == (iota((n * n, block), 1) >> sr)
    picked = jnp.where(keep, dot(crs[...], spread.astype(bf16), 1, 0), 0.0).astype(bf16)
    rise = jnp.where(
        (iota((block, n * n), 0) >> sr) == (iota((block, n * n), 1) >> sn), 1.0, 0.0).astype(bf16)
    same = (iota((block, block), 0) & (rows - 1)) == (iota((block, block), 1) & (rows - 1))
    wf[...] = jnp.where(same, dot(rise, picked, 1, 0), 0.0).astype(bf16)

    follow(1)

    arrive(0)

    def backward(c):
        bk[:, c] = dot(wf[...], rg[:, c], 0, 0).astype(bf16)

    columns(whole, backward)
    own(bk, rb)
    follow(2)

    def forward(c):
        gt[:, c] = dot(wf[...], rm[:, c], 1, 0).astype(bf16)

    arrive(1)
    columns(left, forward)
    follow(3)

    def layer_peer(d):
        return lax.rem(qq + d, LAYER)

    def z_peer(bit):
        size = 1 << bit
        other = zz + size - 2 * size * lax.rem(lax.div(zz, size), 2)
        return other * LAYER + qq

    def ar_copy(stage, d, src, dst, device):
        return pltpu.make_async_remote_copy(
            src_ref=src, dst_ref=dst,
            send_sem=ar_send.at[stage, d - 1], recv_sem=ar_recv.at[stage, d - 1],
            device_id={"seq": device}, device_id_type=pl.DeviceIdType.MESH,
        )

    arrive(2)
    pb[...] = dot(rb[...], pm[...], 1, 1)
    one = [ar_copy(0, d, pb.at[at(layer_peer(d), lrows)], s1.at[d - 1], zz * LAYER + layer_peer(d))
           for d in range(1, LAYER)]
    for c in one:
        c.start()

    def back_signal(c):
        os[:, c] = dot(bp[...], rb[:, c], 0, 0).astype(bf16)

    columns(whole, back_signal)
    store_sig = pltpu.make_async_copy(os, out_sig, local.at[0])
    store_sig.start()
    for c in one:
        c.wait_recv()
    ls[...] = pb[at(qq, lrows), :] + s1[0] + s1[1] + s1[2]
    even = lax.rem(zz, 2)
    two = [ar_copy(1, 1, ls.at[at(1 - even, zrows)], s2, z_peer(0))]
    two[0].start()

    follow(4)

    two[0].wait_recv()
    ms[0] = ls[at(even, zrows), :] + s2[...]

    def swap(bit):
        return ar_copy(1 + bit, 1, ms.at[bit - 1], s3.at[bit - 1], z_peer(bit))

    swaps = [swap(bit) for bit in range(1, log2(nz))]
    swaps[0].start()

    arrive(3)
    for i, c in enumerate(swaps):
        c.wait_recv()
        ms[i + 1] = ms[i] + s3[i]
        if i + 1 < len(swaps):
            swaps[i + 1].start()
    mine = at(qq * 2 + even, zrows)
    gb[mine, :] = ms[len(swaps)] * (1.0 / math.sqrt(n * width))
    after = 1 + log2(nz)
    three = [ar_copy(after, 1, gb.at[mine], gb.at[mine], z_peer(0))]
    three[0].start()

    columns(right, forward)
    own(gt, rt)
    follow(5)

    three[0].wait_recv()
    layer = at(qq, lrows)
    four = [ar_copy(after + 1, d, gb.at[layer], gb.at[layer], zz * LAYER + layer_peer(d))
            for d in range(1, LAYER)]
    for c in four:
        c.start()

    hb = block // 2
    for h in range(2):
        pairs = dot(rg[pl.ds(h * hb, hb), :], rm[...], 1, 1)
        match = (iota((hb, block), 0) & (rows - 1)) == (iota((hb, block), 1) & (rows - 1))
        pairs = jnp.where(match, pairs, 0.0).reshape(hb // rows, rows, block).sum(axis=1)
        pairs = jnp.broadcast_to(pairs[:, None, :], (n // 2, n, block)).reshape(n * n // 2, block)
        pairs = jnp.where(keep[: n * n // 2], pairs, 0.0)
        narrow = lax.dot_general(
            pairs, spread, (((1,), (1,)), ((), ())),
            precision=lax.Precision.HIGHEST, preferred_element_type=f32)
        gc[pl.ds(h * (n * n // 2), n * n // 2), :] = narrow * (1.0 / math.sqrt(width))
    store_cross = pltpu.make_async_copy(gc, out_cross, local.at[1])
    store_cross.start()
    def finish(r, part):
        c = pl.ds(*part)
        rt[r, c] = (cot[r, c].astype(f32) * rt[r, c].astype(f32)).astype(bf16)

    def close(phase):
        part = phases[phase][2]
        finish(at(me), part)
        stored(phase, 0).start()

        def last(k):
            remote(phase, k).wait_recv()
            finish(at(lax.rem(me + n - k, n)), part)
            stored(phase, k).start()

        each(last)

    def stored(phase, k):
        r, c = at(lax.rem(me + n - k, n)), pl.ds(*phases[phase][2])
        return pltpu.make_async_copy(rt.at[r, c], out_gate.at[r, c], closing.at[phase - 4, k])

    close(4)
    for c in four:
        c.wait_recv()
    store_block = pltpu.make_async_copy(gb, out_block, local.at[2])
    store_block.start()
    close(5)

    def drain(k):
        for phase in (4, 5):
            remote(phase, k).wait_send()
            stored(phase, k).wait()

    for phase in (4, 5):
        stored(phase, 0).wait()
    each(drain)
    for c in one + two + swaps + three + four:
        c.wait_send()
    for c in (store_sig, store_cross, store_block):
        c.wait()


def write_kernel(count, *refs):
    copies = [pltpu.make_async_copy(src, dst, refs[-1].at[i])
              for i, (src, dst) in enumerate(zip(refs[:count], refs[count:]))]
    for c in copies:
        c.start()
    for c in copies:
        c.wait()


def write(*arrays):
    free = pl.BlockSpec(memory_space=pl.ANY)
    return pl.pallas_call(
        functools.partial(write_kernel, len(arrays)),
        out_shape=tuple(jax.ShapeDtypeStruct(x.shape, x.dtype) for x in arrays),
        in_specs=[free] * len(arrays),
        out_specs=(free,) * len(arrays),
        scratch_shapes=[pltpu.SemaphoreType.DMA((len(arrays),))],
        compiler_params=pltpu.CompilerParams(vmem_limit_bytes=1 << 20),
    )(*arrays)


def fused(signal, gate_input, cotangent, block_factor, cross_factor, order_table):
    f32, bf16 = jnp.float32, jnp.bfloat16
    n = lax.axis_size("seq")
    block, width = signal.shape
    rows = block // n
    nz = n // LAYER
    crs = cross_factor.transpose(1, 2, 0).reshape(n * n, rows)
    full = pltpu.VMEM((block, width), bf16)
    square = pltpu.VMEM((block, block), bf16)
    free = pl.BlockSpec(memory_space=pl.ANY)
    inputs = (gate_input, cotangent, signal, order_table.reshape(1, block), block_factor, crs)
    steps = 3 + log2(nz)
    results = pl.pallas_call(
        functools.partial(exchange_kernel, n),
        out_shape=(
            jax.ShapeDtypeStruct((block, width), bf16),
            jax.ShapeDtypeStruct((block, width), bf16),
            jax.ShapeDtypeStruct((block, block), f32),
            jax.ShapeDtypeStruct((n * n, rows), f32),
        ),
        in_specs=[pl.BlockSpec(memory_space=pltpu.HBM)] * 6,
        out_specs=(free,) * 4,
        scratch_shapes=[pltpu.VMEM(x.shape, x.dtype) for x in inputs]
        + [full] * 10 + [square] * 3 + [
            pltpu.VMEM((block, block), f32),
            pltpu.VMEM((LAYER - 1, block // LAYER, block), f32),
            pltpu.VMEM((block // LAYER, block), f32),
            pltpu.VMEM((block // LAYER // 2, block), f32),
            pltpu.VMEM((log2(nz), block // LAYER // 2, block), f32),
            pltpu.VMEM((log2(nz) - 1, block // LAYER // 2, block), f32),
            pltpu.VMEM((block, block), f32),
            pltpu.VMEM((n * n, rows), f32),
            pltpu.SemaphoreType.DMA((6, n - 1)),
            pltpu.SemaphoreType.DMA((6, n - 1)),
            pltpu.SemaphoreType.DMA((steps, LAYER - 1)),
            pltpu.SemaphoreType.DMA((steps, LAYER - 1)),
            pltpu.SemaphoreType.DMA((6,)),
            pltpu.SemaphoreType.DMA((2, n)),
        ],
        compiler_params=pltpu.CompilerParams(
            collective_id=0, has_side_effects=True, vmem_limit_bytes=40 << 20),
    )(*(pltpu.with_memory_space_constraint(x, pltpu.HBM) for x in inputs))
    grad_signal, grad_gate, grad_block, pairs = write(*results)
    grad_cross = pairs.reshape(n, n, rows).transpose(2, 0, 1)
    return (grad_signal, grad_gate, grad_block, grad_cross)


def per_device(signal, gate_input, cotangent, block_factor, cross_factor, order_table):
    f32 = jnp.float32
    bf16 = jnp.bfloat16
    count = lax.axis_size("seq")
    width = signal.shape[1]
    permuted = jnp.take(signal, order_table, axis=0)
    mixed = jnp.dot(block_factor, permuted, preferred_element_type=f32).astype(bf16)
    gate_grad = (cotangent.astype(f32) * gate_input.astype(f32)).astype(bf16)
    spread_mixed = lax.all_to_all(mixed[None], "seq", split_axis=1, concat_axis=0, tiled=True)
    spread_grad = lax.all_to_all(gate_grad[None], "seq", split_axis=1, concat_axis=0, tiled=True)
    gated = jnp.einsum(
        "cij,jcd->icd", cross_factor, spread_mixed, preferred_element_type=f32
    ).astype(bf16)
    gated_home = lax.all_to_all(gated, "seq", split_axis=0, concat_axis=1, tiled=True)
    grad_cross = jnp.einsum(
        "icd,jcd->cij", spread_grad, spread_mixed, preferred_element_type=f32
    ) / math.sqrt(width)
    back = jnp.einsum("cij,icd->jcd", cross_factor, spread_grad, preferred_element_type=f32).astype(
        bf16
    )
    back_home = lax.all_to_all(back, "seq", split_axis=0, concat_axis=1, tiled=True)
    grad_gate = (cotangent.astype(f32) * gated_home[0].astype(f32)).astype(bf16)
    back_rows = back_home[0]
    partial_block = lax.dot_general(
        back_rows, permuted, (((1,), (1,)), ((), ())), preferred_element_type=f32
    )
    grad_block = lax.psum(partial_block, "seq") / math.sqrt(count * width)
    spread = lax.dot_general(
        block_factor, back_rows, (((0,), (0,)), ((), ())), preferred_element_type=f32
    ).astype(bf16)
    grad_signal = jnp.zeros_like(spread).at[order_table].set(spread)
    return (grad_signal, grad_gate, grad_block, grad_cross)


def solution(mesh):
    in_specs = (
        P(("groups", "seq"), None),
        P(("groups", "seq"), None),
        P(("groups", "seq"), None),
        P(),
        P("seq", None, None),
        P(),
    )
    out_specs = (
        P(("groups", "seq"), None),
        P(("groups", "seq"), None),
        P("groups", None),
        P("seq", "groups", None),
    )

    def body(signal, *rest):
        n = mesh.shape["seq"]
        block = signal.shape[0]
        whole = block % n == 0 and (block // n) % 16 == 0 and n % (4 * LAYER) == 0
        whole = whole and n & (n - 1) == 0 and block & (block - 1) == 0
        return (fused if whole else per_device)(signal, *rest)

    return jax.shard_map(body, mesh=mesh, in_specs=in_specs, out_specs=out_specs, check_vma=False)
```
